256 devices in a mesh: sub: 32 (over x, z), col: 8 (over y, core).
Axes of the slice: x: 4, y: 4, z: 8, core: 2. Of those that a mesh axis runs over, the one named last changes fastest.
Arguments:
- leaf_basis: bfloat16 [32, 8, 2048, 512], P('sub', 'col'), as said below
- transfers: bfloat16 [32, 8, 4, 512, 512], P('sub', 'col'), as said below
- couplings: bfloat16 [32, 8, 6, 512, 512], P('sub', 'col'), may hold values from -0.25 to 0.25
- partners: int32 [32, 8, 6], P('sub', 'col'), may hold values from 0 to 7
Outputs:
- q_leaf: bfloat16 [32, 8, 2048, 512], P('sub', 'col')
- root_triangle: bfloat16 [32, 8, 512, 512], P('sub', 'col')
- coupled: bfloat16 [32, 8, 6, 512, 512], P('sub', 'col')
The draws below stay inside these ranges and needn't reach their ends.
Inputs may be any that keep to these rules, and one draw needn't show every extreme that they name: partners[s,c,k] names the leaf cluster (s, partners[s,c,k]) as column cluster; entries may repeat. Every transfer matrix is a positive diagonal plus a dense part; transfers[s,c,l] is equal for all s with the same s >> l. `leaf_basis`: every leaf basis has full column rank.
All inputs are finite; a program needn't handle non-finite values.
Results may differ from the reference program's by a relative error of at most 0.0063.
Values may be sent and summed in bfloat16 or wider, within the bound.
No kernel may reach another device: no remote copies, remote signals or barrier semaphores. Data moves between devices by JAX's collectives and lax.ppermute only.
A program may use at most 128 MiB of HBM per device.

```python
import jax
import jax.numpy as jnp
import numpy as np
from jax import lax

LEAF = 2048
RANK = 512
SLOTS = 6
LEVELS = 4
SUBS = 32
COLS = 8


def draw_leaf_basis(key, part):
    base_key = jax.random.fold_in(key, 5)
    first_key, second_key = jax.random.split(base_key, 2)
    shape = (SUBS, COLS, LEAF, RANK)
    own = jax.random.normal(first_key, shape, jnp.float32)
    common = jax.random.normal(second_key, (SUBS, COLS, LEAF, 1), jnp.float32)
    mixed = 0.8 * own + 0.6 * common
    mixed = jnp.clip(mixed, -5.0, 5.0)
    return (mixed / jnp.sqrt(1.0 * LEAF)).astype(jnp.bfloat16)


def draw_transfers(key, part):
    identity = jnp.eye(RANK, dtype=jnp.float32)
    levels_list = []
    for level_index in range(LEVELS):
        level_key = jax.random.fold_in(key, 17 + level_index)
        first_key, second_key = jax.random.split(level_key)
        clusters = SUBS >> level_index
        shape = (clusters, COLS, RANK, RANK)
        diagonal = jnp.exp(jax.random.uniform(first_key, (clusters, COLS, RANK), jnp.float32, jnp.log(0.6), jnp.log(1.6)))
        dense = 0.3 * jax.random.normal(second_key, shape, jnp.float32) / jnp.sqrt(1.0 * RANK)
        matrix = dense + diagonal[..., None] * identity
        levels_list.append(jnp.repeat(matrix, 1 << level_index, axis=0))
    return jnp.stack(levels_list, axis=2).astype(jnp.bfloat16)


def touch_ends(array, key, least, high):
    longest = array.shape.index(max(array.shape))
    spots = []
    for shift in (0, 1):
        where = [jax.random.randint(jax.random.fold_in(key, axis), (), 0, length) for axis, length in enumerate(array.shape)]
        where[longest] = (where[longest] + shift) % array.shape[longest]
        spots.append(tuple(where))
    return array.at[spots[0]].set(least).at[spots[1]].set(high)


def level_of(rng, extent, shards, smallest, top_value):
    gain = 1.0
    for dim, blocks in shards:
        steps = jax.random.uniform(jax.random.fold_in(jax.random.fold_in(rng, 6), dim), (blocks,), jnp.float32, smallest / len(shards), top_value / len(shards))
        gain = gain * jnp.repeat(jnp.exp(steps), extent[dim] // blocks).reshape((-1,) + (1,) * (len(extent) - 1 - dim))
    return gain


def normal_values(key, shape, spread, most, shards=(), kind=jnp.bfloat16):
    level = level_of(key, shape, shards, -0.22, 0.18) if shards else 1.0
    result = jax.random.normal(key, shape, jnp.float32) * spread * level
    return jnp.minimum(jnp.maximum(result, -most), most).astype(kind)


def setup_inputs(seed: int = 0) -> dict:
    seeds = jax.random.split(jax.random.key(seed), 5)
    leaf_basis = draw_leaf_basis(jax.random.fold_in(seeds[4], 71), 0)
    transfers = draw_transfers(jax.random.fold_in(seeds[4], 71), 0)
    couplings = normal_values(seeds[2], (SUBS, COLS, SLOTS, RANK, RANK), RANK ** -0.5, 0.25, ((0, 32), (1, 8)))
    partners = touch_ends(jax.random.randint(seeds[3], (SUBS, COLS, SLOTS), 0, COLS), jax.random.fold_in(seeds[3], 1), 0, COLS - 1).astype(jnp.int32)
    return dict(leaf_basis=leaf_basis, transfers=transfers, couplings=couplings, partners=partners)


highest = lax.Precision.HIGHEST

def reference(leaf_basis, transfers, couplings, partners):
    basis_wide = leaf_basis.astype(jnp.float32)
    gram_leaf = jnp.einsum('scia,scib->scab', basis_wide, basis_wide, precision=highest)
    lower_leaf = jnp.linalg.cholesky(gram_leaf)
    q_transposed = lax.linalg.triangular_solve(lower_leaf, jnp.swapaxes(basis_wide, -1, -2), left_side=True, lower=True)
    q_leaf = jnp.swapaxes(q_transposed, -1, -2).astype(jnp.bfloat16)
    triangle = jnp.swapaxes(lower_leaf, -1, -2)
    rounded = triangle.astype(jnp.bfloat16)
    left_product = jnp.einsum('scab,sckbd->sckad', rounded.astype(jnp.float32), couplings.astype(jnp.float32), precision=highest).astype(jnp.bfloat16)
    sub_index = jnp.arange(SUBS, dtype=jnp.int32)[:, None, None]
    chosen = rounded[sub_index, partners]
    coupled = jnp.einsum('sckab,sckdb->sckad', left_product.astype(jnp.float32), chosen.astype(jnp.float32), precision=highest).astype(jnp.bfloat16)
    current = triangle
    for level_index in range(LEVELS):
        flipped = np.arange(SUBS) ^ 1 << level_index
        moved = jnp.einsum('scab,scbd->scad', current, transfers[:, :, level_index].astype(jnp.float32), precision=highest)
        partner_block = moved[flipped]
        gram_matrix = jnp.einsum('scba,scbd->scad', moved, moved, precision=highest) + jnp.einsum('scba,scbd->scad', partner_block, partner_block, precision=highest)
        current = jnp.swapaxes(jnp.linalg.cholesky(gram_matrix), -1, -2)
    root_triangle = current.astype(jnp.bfloat16)
    return (q_leaf, root_triangle, coupled)
```

```python
import jax
import jax.numpy as jnp
from jax import lax
from jax.experimental import pallas as pl
from jax.experimental.pallas import tpu as pltpu
from jax.sharding import PartitionSpec as P

f32, bf16 = jnp.float32, jnp.bfloat16
NN = ((1,), (0,))
TN = ((0,), (0,))
NT = ((1,), (1,))
SIDE = 128


def split(a):
    high = a.astype(bf16)
    return high, (a - high.astype(f32)).astype(bf16)


def dot(a, b, dims):
    return lax.dot_general(a, b, (dims, ((), ())), preferred_element_type=f32)


def dot3(a, b, dims):
    a_high, a_low = split(a)
    b_high, b_low = split(b)
    return dot(a_high, b_high, dims) + (dot(a_high, b_low, dims) + dot(a_low, b_high, dims))


def invert_lower(block):
    n = block.shape[0]
    parts = n // 8
    lane = lax.broadcasted_iota(jnp.int32, (8, n), 1)
    sub = lax.broadcasted_iota(jnp.int32, (8, n), 0)
    rows = [block[8 * t : 8 * t + 8, :] for t in range(parts)]
    result = []
    wide = lambda v: jnp.broadcast_to(v, (8, n))
    for t in range(parts):
        here = (lane >= 8 * t) & (lane < 8 * t + 8)
        current = rows[t]
        cols = [wide(current[:, 8 * t + k : 8 * t + k + 1]) for k in range(8)]
        work = jnp.where(here, (lane == sub + 8 * t).astype(f32), current)
        done = jnp.zeros((8, n), f32)
        scale = jnp.zeros((8, n), f32)
        for j in range(8):
            root = lax.rsqrt(wide(cols[j][j : j + 1, :]))
            inverse = root * root
            factor = jnp.where(sub == j, 0.0, cols[j]) * inverse
            pivot = wide(work[j : j + 1, :])
            done = jnp.where(sub == j, pivot * root, done)
            scale = jnp.where(sub == j, inverse, scale)
            work = work - factor * pivot
            for k in range(j + 1, 8):
                cols[k] = cols[k] - factor * wide(cols[k][j : j + 1, :])
        result.append(jnp.where(lane < 8 * t + 8, done, 0.0))
        if t + 1 < parts:
            scaled = work * scale
            lines = [wide(scaled[k : k + 1, :]) for k in range(8)]
            for s in range(t + 1, parts):
                total = jnp.where(here, 0.0, rows[s])
                for k in range(8):
                    total = total - wide(rows[s][:, 8 * t + k : 8 * t + k + 1]) * lines[k]
                rows[s] = total
    return jnp.concatenate(result, axis=0)


def factor_steps(x_ref, put_triangle, put_inverse):
    n = x_ref.shape[0]
    lane = lax.broadcasted_iota(jnp.int32, (SIDE, n), 1)
    sub = lax.broadcasted_iota(jnp.int32, (SIDE, n), 0)
    all_lane = lax.broadcasted_iota(jnp.int32, (n, n), 1)
    all_sub = lax.broadcasted_iota(jnp.int32, (n, n), 0)

    def step(k, carry):
        start = pl.multiple_of(k * SIDE, SIDE)
        at = pl.ds(start, SIDE)
        lower_inverse = invert_lower(x_ref[at, at])
        row = x_ref[at, :]
        here = (lane >= start) & (lane < start + SIDE)
        panel = dot3(lower_inverse, jnp.where(here, (lane == sub + start).astype(f32), row), NN)
        if put_inverse is not None:
            put_inverse(at, jnp.where(lane <= sub + start, panel, 0.0))
        put_triangle(at, jnp.where(lane >= sub + start, dot3(lower_inverse, row, NN), 0.0))
        change = dot3(jnp.where(lane >= start + SIDE, panel, 0.0), panel, TN)
        clear = (all_lane >= start) & (all_lane < start + SIDE) & (all_sub >= start + SIDE)
        x_ref[...] = jnp.where(clear, 0.0, x_ref[...]) - change
        return carry

    lax.fori_loop(0, n // SIDE, step, 0)


def leaf_kernel(gram_ref, rounded_ref, high_ref, low_ref, x_ref):
    x_ref[...] = gram_ref[...]

    def put_triangle(at, value):
        rounded_ref[at, :] = value.astype(bf16)

    def put_inverse(at, value):
        high, low = split(value)
        high_ref[at, :] = high
        low_ref[at, :] = low

    factor_steps(x_ref, put_triangle, put_inverse)


def root_kernel(gram_ref, root_ref, x_ref):
    x_ref[...] = gram_ref[...]

    def put_triangle(at, value):
        root_ref[at, :] = value.astype(bf16)

    factor_steps(x_ref, put_triangle, None)


def gram_kernel(basis_ref, transfer_ref, gram_ref, moved_ref):
    basis = basis_ref[...]
    gram = dot(basis, basis, TN)
    gram_ref[...] = gram
    path = transfer_ref[0].astype(f32)
    for level in range(1, transfer_ref.shape[0]):
        high, low = split(path)
        step = transfer_ref[level]
        path = dot(high, step, NN)
        if level > 1:
            path = path + dot(low, step, NN)
    moved_ref[...] = dot3(path, dot3(gram, path, NN), TN)


def basis_kernel(basis_ref, high_ref, low_ref, q_ref):
    basis = basis_ref[...]
    q_ref[...] = (dot(basis, high_ref[...], NT) + dot(basis, low_ref[...], NT)).astype(bf16)


def left_kernel(rounded_ref, block_ref, left_ref):
    left_ref[0] = dot(rounded_ref[...], block_ref[0], NN).astype(bf16)


def right_kernel(partner_ref, left_ref, chosen_ref, out_ref):
    del partner_ref
    out_ref[0] = dot(left_ref[0], chosen_ref[0], NT).astype(bf16)


def shards(leaf_basis, transfers, couplings, partners):
    basis, steps, blocks, picks = leaf_basis[0, 0], transfers[0, 0], couplings[0, 0], partners[0, 0]
    leaf, rank = basis.shape
    slots = blocks.shape[0]
    square = lambda dtype: jax.ShapeDtypeStruct((rank, rank), dtype)
    work = pltpu.VMEM((rank, rank), f32)
    gram, moved = pl.pallas_call(gram_kernel, out_shape=(square(f32), square(f32)), name="gram")(basis, steps)

    count = lax.axis_size("sub")
    group = 1 << steps.shape[0]
    groups = [list(range(low, low + group)) for low in range(0, count, group)]
    top = lax.psum(moved, "sub", axis_index_groups=groups)

    rounded, high, low = pl.pallas_call(
        leaf_kernel, out_shape=(square(bf16), square(bf16), square(bf16)), scratch_shapes=[work], name="leaf"
    )(gram)
    pieces = lax.all_gather(rounded, "col", axis=0)

    chunk = leaf // 4
    q_leaf = pl.pallas_call(
        basis_kernel,
        grid=(leaf // chunk,),
        in_specs=[
            pl.BlockSpec((chunk, rank), lambda i: (i, 0)),
            pl.BlockSpec((rank, rank), lambda i: (0, 0)),
            pl.BlockSpec((rank, rank), lambda i: (0, 0)),
        ],
        out_specs=pl.BlockSpec((chunk, rank), lambda i: (i, 0)),
        out_shape=jax.ShapeDtypeStruct((leaf, rank), bf16),
        name="basis",
    )(basis, high, low)
    left = pl.pallas_call(
        left_kernel,
        grid=(slots,),
        in_specs=[
            pl.BlockSpec((rank, rank), lambda k: (0, 0)),
            pl.BlockSpec((1, rank, rank), lambda k: (k, 0, 0)),
        ],
        out_specs=pl.BlockSpec((1, rank, rank), lambda k: (k, 0, 0)),
        out_shape=jax.ShapeDtypeStruct(blocks.shape, bf16),
        name="left",
    )(rounded, blocks)
    root = pl.pallas_call(root_kernel, out_shape=square(bf16), scratch_shapes=[work], name="root")(top)
    coupled = pl.pallas_call(
        right_kernel,
        grid_spec=pltpu.PrefetchScalarGridSpec(
            num_scalar_prefetch=1,
            grid=(slots,),
            in_specs=[
                pl.BlockSpec((1, rank, rank), lambda k, pick: (k, 0, 0)),
                pl.BlockSpec((1, rank, rank), lambda k, pick: (pick[k], 0, 0)),
            ],
            out_specs=pl.BlockSpec((1, rank, rank), lambda k, pick: (k, 0, 0)),
        ),
        out_shape=jax.ShapeDtypeStruct(blocks.shape, bf16),
        name="right",
    )(picks, left, pieces)
    return (q_leaf[None, None], root[None, None], coupled[None, None])


def solution(mesh):
    in_specs = (
        P("sub", "col", None, None),
        P("sub", "col", None, None, None),
        P("sub", "col", None, None, None),
        P("sub", "col", None),
    )
    out_specs = (
        P("sub", "col", None, None),
        P("sub", "col", None, None),
        P("sub", "col", None, None, None),
    )
    return jax.shard_map(shards, mesh=mesh, in_specs=in_specs, out_specs=out_specs, check_vma=False)
```

```python
import jax
import jax.numpy as jnp
from jax import lax
from jax.experimental import pallas as pl
from jax.experimental.pallas import tpu as pltpu
from jax.sharding import PartitionSpec as P

f32, bf16 = jnp.float32, jnp.bfloat16
NN = ((1,), (0,))
TN = ((0,), (0,))
NT = ((1,), (1,))
SIDE = 128
BASE = 16


def split(a):
    high = a.astype(bf16)
    return high, (a - high.astype(f32)).astype(bf16)


def dot(a, b, dims):
    return lax.dot_general(a, b, (dims, ((), ())), preferred_element_type=f32)


def dot3(a, b, dims):
    a_high, a_low = split(a)
    b_high, b_low = split(b)
    return dot(a_high, b_high, dims) + (dot(a_high, b_low, dims) + dot(a_low, b_high, dims))


def lane_of(rows, column):
    return jnp.take_along_axis(rows, jnp.full(rows.shape, column, jnp.int32), axis=1)


def invert_lower(block):
    n = block.shape[0]
    parts = n // 8
    per = BASE // 8
    lane = lax.broadcasted_iota(jnp.int32, (8, n), 1)
    sub = lax.broadcasted_iota(jnp.int32, (8, n), 0)
    rows = [block[8 * t : 8 * t + 8, :] for t in range(parts)]
    result = []
    wide = lambda v: jnp.broadcast_to(v, (8, n))
    for first in range(0, parts, per):
        group = range(first, first + per)
        final = first + per >= parts
        for t in group:
            here = (lane >= 8 * t) & (lane < 8 * t + 8)
            cols = [lane_of(rows[t], 8 * t + k) for k in range(8)]
            work = jnp.where(here, (lane == sub + 8 * t).astype(f32), rows[t])
            done = jnp.zeros((8, n), f32)
            scale = jnp.zeros((8, n), f32)
            for j in range(8):
                root = lax.rsqrt(wide(cols[j][j : j + 1, :]))
                inverse = root * root
                factor = jnp.where(sub == j, 0.0, cols[j]) * inverse
                pivot = wide(work[j : j + 1, :])
                done = jnp.where(sub == j, pivot * root, done)
                scale = jnp.where(sub == j, inverse, scale)
                work = work - factor * pivot
                for k in range(j + 1, 8):
                    cols[k] = cols[k] - factor * wide(cols[k][j : j + 1, :])
            result.append(jnp.where(lane < 8 * t + 8, done, 0.0))
            if t + 1 == parts:
                break
            rows[t] = work * scale
            lines = [wide(rows[t][k : k + 1, :]) for k in range(8)]
            for s in group:
                if s == t or (final and s < t):
                    continue
                total = jnp.where(here, 0.0, rows[s])
                for k in range(8):
                    total = total - lane_of(rows[s], 8 * t + k) * lines[k]
                rows[s] = total
        if not final:
            low, high = 8 * first, 8 * (first + per)
            solved = jnp.concatenate([rows[t] for t in group], axis=0)
            rest = jnp.concatenate(rows[first + per :], axis=0)
            lanes = lax.broadcasted_iota(jnp.int32, rest.shape, 1)
            change = dot3(rest[:, low:high], solved, NN)
            rest = jnp.where((lanes >= low) & (lanes < high), 0.0, rest) - change
            for i in range(first + per, parts):
                at = 8 * (i - first - per)
                rows[i] = rest[at : at + 8, :]
    return jnp.concatenate(result, axis=0)


def factor_steps(x_ref, put_triangle, put_inverse):
    n = x_ref.shape[0]
    lane = lax.broadcasted_iota(jnp.int32, (SIDE, n), 1)
    sub = lax.broadcasted_iota(jnp.int32, (SIDE, n), 0)
    all_lane = lax.broadcasted_iota(jnp.int32, (n, n), 1)
    all_sub = lax.broadcasted_iota(jnp.int32, (n, n), 0)

    def step(k, carry):
        start = pl.multiple_of(k * SIDE, SIDE)
        at = pl.ds(start, SIDE)
        lower_inverse = invert_lower(x_ref[at, at])
        row = x_ref[at, :]
        here = (lane >= start) & (lane < start + SIDE)
        panel = dot3(lower_inverse, jnp.where(here, (lane == sub + start).astype(f32), row), NN)
        if put_inverse is not None:
            put_inverse(at, jnp.where(lane <= sub + start, panel, 0.0))
        put_triangle(at, jnp.where(lane >= sub + start, dot3(lower_inverse, row, NN), 0.0))
        change = dot3(jnp.where(lane >= start + SIDE, panel, 0.0), panel, TN)
        clear = (all_lane >= start) & (all_lane < start + SIDE) & (all_sub >= start + SIDE)
        x_ref[...] = jnp.where(clear, 0.0, x_ref[...]) - change
        return carry

    lax.fori_loop(0, n // SIDE, step, 0)


def corners(n):
    count = n // SIDE
    return [(i, j) for i in range(count) for j in range(i, count)]


def leaf_kernel(gram_ref, rounded_ref, packed_ref, high_ref, low_ref, x_ref):
    x_ref[...] = gram_ref[...]

    def put_triangle(at, value):
        rounded_ref[at, :] = value.astype(bf16)

    def put_inverse(at, value):
        high, low = split(value)
        high_ref[at, :] = high
        low_ref[at, :] = low

    factor_steps(x_ref, put_triangle, put_inverse)
    for number, (i, j) in enumerate(corners(gram_ref.shape[0])):
        block = rounded_ref[i * SIDE : (i + 1) * SIDE, j * SIDE : (j + 1) * SIDE]
        packed_ref[number * SIDE : (number + 1) * SIDE, :] = block


def root_kernel(packed_ref, root_ref, x_ref):
    for number, (i, j) in enumerate(corners(x_ref.shape[0])):
        block = packed_ref[number * SIDE : (number + 1) * SIDE, :]
        x_ref[i * SIDE : (i + 1) * SIDE, j * SIDE : (j + 1) * SIDE] = block
        if i != j:
            x_ref[j * SIDE : (j + 1) * SIDE, i * SIDE : (i + 1) * SIDE] = jnp.zeros((SIDE, SIDE), f32)

    def put_triangle(at, value):
        root_ref[at, :] = value.astype(bf16)

    factor_steps(x_ref, put_triangle, None)


def gram_kernel(basis_ref, transfer_ref, gram_ref, moved_ref):
    basis = basis_ref[...]
    gram = dot(basis, basis, TN)
    gram_ref[...] = gram
    path = transfer_ref[0].astype(f32)
    for level in range(1, transfer_ref.shape[0]):
        high, low = split(path)
        step = transfer_ref[level]
        path = dot(high, step, NN)
        if level > 1:
            path = path + dot(low, step, NN)
    n = gram.shape[0]
    half = n // 2
    carried = dot3(gram, path, NN)
    upper = dot3(path[:, :half], carried, TN)
    lower = dot3(path[:, half:], carried[:, half:], TN)
    for number, (i, j) in enumerate(corners(n)):
        if i * SIDE < half:
            block = upper[i * SIDE : (i + 1) * SIDE, j * SIDE : (j + 1) * SIDE]
        else:
            block = lower[i * SIDE - half : (i + 1) * SIDE - half, j * SIDE - half : (j + 1) * SIDE - half]
        moved_ref[number * SIDE : (number + 1) * SIDE, :] = block


def basis_kernel(basis_ref, high_ref, low_ref, q_ref):
    basis = basis_ref[...]
    q_ref[...] = (dot(basis, high_ref[...], NT) + dot(basis, low_ref[...], NT)).astype(bf16)


def left_kernel(rounded_ref, block_ref, left_ref):
    half = rounded_ref.shape[0] // 2
    left_ref[0, :half, :] = dot(rounded_ref[:half, :], block_ref[0], NN).astype(bf16)
    left_ref[0, half:, :] = dot(rounded_ref[half:, half:], block_ref[0, half:, :], NN).astype(bf16)


def right_kernel(place_ref, left_ref, mine_ref, other_ref, out_ref, full_ref):
    n = full_ref.shape[0]
    half = n // 2
    swapped = place_ref[1, pl.program_id(0)] != 0
    for number, (i, j) in enumerate(corners(n)):
        at = slice(number * SIDE, (number + 1) * SIDE)
        block = jnp.where(swapped, other_ref[0, at, :], mine_ref[0, at, :])
        full_ref[i * SIDE : (i + 1) * SIDE, j * SIDE : (j + 1) * SIDE] = block
        if i != j:
            full_ref[j * SIDE : (j + 1) * SIDE, i * SIDE : (i + 1) * SIDE] = jnp.zeros((SIDE, SIDE), bf16)
    out_ref[0, :, :half] = dot(left_ref[0], full_ref[:half, :], NT).astype(bf16)
    out_ref[0, :, half:] = dot(left_ref[0, :, half:], full_ref[half:, half:], NT).astype(bf16)


def shards(leaf_basis, transfers, couplings, partners):
    basis, steps, blocks, picks = leaf_basis[0, 0], transfers[0, 0], couplings[0, 0], partners[0, 0]
    leaf, rank = basis.shape
    slots = blocks.shape[0]
    square = lambda dtype: jax.ShapeDtypeStruct((rank, rank), dtype)
    tall = len(corners(rank)) * SIDE
    packed_shape = lambda dtype: jax.ShapeDtypeStruct((tall, SIDE), dtype)
    work = pltpu.VMEM((rank, rank), f32)
    gram, moved = pl.pallas_call(gram_kernel, out_shape=(square(f32), packed_shape(f32)), name="gram")(basis, steps)

    count = lax.axis_size("sub")
    group = 1 << steps.shape[0]
    groups = [list(range(low, low + group)) for low in range(0, count, group)]
    shares = lax.all_to_all(moved.reshape(group, tall // group, SIDE), "sub", 0, 0, axis_index_groups=groups)
    rounded, packed, high, low = pl.pallas_call(
        leaf_kernel,
        out_shape=(square(bf16), packed_shape(bf16), square(bf16), square(bf16)),
        scratch_shapes=[work],
        name="leaf",
    )(gram)
    shares, rounded, packed, high, low = lax.optimization_barrier((shares, rounded, packed, high, low))
    share = jnp.sum(shares, axis=0)
    top = lax.all_to_all(jnp.broadcast_to(share, shares.shape), "sub", 0, 0, axis_index_groups=groups)
    top = top.reshape(tall, SIDE)

    columns = lax.axis_size("col")
    mine = [packed]
    for shift in range(2, columns, 2):
        mine.append(lax.ppermute(packed, "col", [(i, (i - shift) % columns) for i in range(columns)]))
    chunk = leaf // 4
    q_leaf = pl.pallas_call(
        basis_kernel,
        grid=(leaf // chunk,),
        in_specs=[
            pl.BlockSpec((chunk, rank), lambda i: (i, 0)),
            pl.BlockSpec((rank, rank), lambda i: (0, 0)),
            pl.BlockSpec((rank, rank), lambda i: (0, 0)),
        ],
        out_specs=pl.BlockSpec((chunk, rank), lambda i: (i, 0)),
        out_shape=jax.ShapeDtypeStruct((leaf, rank), bf16),
        name="basis",
    )(basis, high, low)
    left = pl.pallas_call(
        left_kernel,
        grid=(slots,),
        in_specs=[
            pl.BlockSpec((rank, rank), lambda k: (0, 0)),
            pl.BlockSpec((1, rank, rank), lambda k: (k, 0, 0)),
        ],
        out_specs=pl.BlockSpec((1, rank, rank), lambda k: (k, 0, 0)),
        out_shape=jax.ShapeDtypeStruct(blocks.shape, bf16),
        name="left",
    )(rounded, blocks)
    top, mine, left, q_leaf = lax.optimization_barrier((top, tuple(mine), left, q_leaf))
    mine = jnp.stack(mine)
    other = lax.ppermute(mine, "col", [(i, i ^ 1) for i in range(columns)])
    top, mine = lax.optimization_barrier((top, mine))
    here = lax.axis_index("col")
    places = jnp.stack([((picks >> 1) - (here >> 1)) & (columns // 2 - 1), (picks ^ here) & 1])
    root = pl.pallas_call(root_kernel, out_shape=square(bf16), scratch_shapes=[work], name="root")(top)
    root, other = lax.optimization_barrier((root, other))
    coupled = pl.pallas_call(
        right_kernel,
        grid_spec=pltpu.PrefetchScalarGridSpec(
            num_scalar_prefetch=1,
            grid=(slots,),
            in_specs=[
                pl.BlockSpec((1, rank, rank), lambda k, place: (k, 0, 0)),
                pl.BlockSpec((1, tall, SIDE), lambda k, place: (place[0, k], 0, 0)),
                pl.BlockSpec((1, tall, SIDE), lambda k, place: (place[0, k], 0, 0)),
            ],
            out_specs=pl.BlockSpec((1, rank, rank), lambda k, place: (k, 0, 0)),
            scratch_shapes=[pltpu.VMEM((rank, rank), bf16)],
        ),
        out_shape=jax.ShapeDtypeStruct(blocks.shape, bf16),
        name="right",
    )(places, left, mine, other)
    return (q_leaf[None, None], root[None, None], coupled[None, None])


def solution(mesh):
    in_specs = (
        P("sub", "col", None, None),
        P("sub", "col", None, None, None),
        P("sub", "col", None, None, None),
        P("sub", "col", None),
    )
    out_specs = (
        P("sub", "col", None, None),
        P("sub", "col", None, None),
        P("sub", "col", None, None, None),
    )
    return jax.shard_map(shards, mesh=mesh, in_specs=in_specs, out_specs=out_specs, check_vma=False)
```

```python
import jax
import jax.numpy as jnp
from jax import lax
from jax.experimental import pallas as pl
from jax.experimental.pallas import tpu as pltpu
from jax.sharding import PartitionSpec as P


f32, bf16 = jnp.float32, jnp.bfloat16
NN = ((1,), (0,))
TN = ((0,), (0,))
NT = ((1,), (1,))
TT = ((0,), (1,))
SIDE = 128


def split(a):
    high = a.astype(bf16)
    return high, (a - high.astype(f32)).astype(bf16)


def dot(a, b, dims):
    return lax.dot_general(a, b, (dims, ((), ())), preferred_element_type=f32)


def product(a, b, dims):
    return dot(a[0], b[0], dims) + (dot(a[0], b[1], dims) + dot(a[1], b[0], dims))


def lane_of(rows, column):
    return jnp.take_along_axis(rows, jnp.full(rows.shape, column, jnp.int32), axis=1)


def invert_lower(block):
    n = block.shape[0]; parts = n // 8
    lane = lax.broadcasted_iota(jnp.int32, (8, n), 1)
    sub = lax.broadcasted_iota(jnp.int32, (8, n), 0)
    rows = [block[8*t:8*t+8, :] for t in range(parts)]
    result = []
    wide = lambda v: jnp.broadcast_to(v, (8, n))

    def pivots(t):
        here = (lane >= 8*t) & (lane < 8*t + 8)
        cols = [lane_of(rows[t], 8*t+k) for k in range(8)]
        work = jnp.where(here, (lane == sub + 8*t).astype(f32), rows[t])
        done = jnp.zeros((8, n), f32); scale = jnp.zeros((8, n), f32)
        for j in range(8):
            root = lax.rsqrt(wide(cols[j][j:j+1, :]))
            factor = jnp.where(sub == j, 0.0, cols[j]) * root
            for k in range(j+1, 8):
                cols[k] = cols[k] - factor * (wide(cols[k][j:j+1, :]) * root)
            pivot = wide(work[j:j+1, :]) * root
            done = jnp.where(sub == j, pivot, done)
            scale = jnp.where(sub == j, root * root, scale)
            work = work - factor * pivot
        result.append(jnp.where(lane < 8*t + 8, done, 0.0))
        rows[t] = work * scale
        return here, [wide(rows[t][k:k+1, :]) for k in range(8)]

    def apply(s, t, here, lines):
        terms = [lane_of(rows[s], 8*t+k) * lines[k] for k in range(8)]
        a = (terms[0] + terms[1]) + (terms[2] + terms[3])
        b = (terms[4] + terms[5]) + (terms[6] + terms[7])
        rows[s] = jnp.where(here, 0.0, rows[s]) - (a + b)

    for t in range(0, parts, 2):
        here, lines = pivots(t)
        apply(t+1, t, here, lines)
        more = t + 2 < parts
        if more: apply(t+2, t, here, lines)
        here, lines = pivots(t+1)
        if more:
            apply(t+2, t+1, here, lines)
            apply(t, t+1, here, lines)
        if t + 3 < parts:
            low, high = 8*t, 8*t+16
            solved = jnp.concatenate([rows[t], rows[t+1]], axis=0)
            rest = jnp.concatenate(rows[t+3:], axis=0)
            ln = lax.broadcasted_iota(jnp.int32, rest.shape, 1)
            change = product(split(rest[:, low:high]), split(solved), NN)
            rest = jnp.where((ln >= low) & (ln < high), 0.0, rest) - change
            for i in range(t+3, parts):
                rows[i] = rest[8*(i-t-3):8*(i-t-3)+8, :]
    return jnp.concatenate(result, axis=0)


def factor(x_ref, put_triangle, put_inverse, beside=None):
    n = x_ref.shape[0]; count = n // SIDE
    sub = lax.broadcasted_iota(jnp.int32, (SIDE, SIDE), 0)
    lane = lax.broadcasted_iota(jnp.int32, (SIDE, SIDE), 1)
    diagonal = x_ref[0:SIDE, 0:SIDE]
    for k in range(count):
        a, b = k*SIDE, (k+1)*SIDE
        if beside is not None:
            beside(k, count)
        inverse = invert_lower(diagonal)
        inv2 = split(inverse)
        put_triangle(k, k, jnp.where(lane >= sub, product(inv2, split(diagonal), NN), 0.0))
        right = []
        for j in range(k+1, count):
            piece = product(inv2, split(x_ref[a:b, j*SIDE:(j+1)*SIDE]), NN)
            put_triangle(k, j, piece)
            right.append(split(piece))
            if j == k+1:
                diagonal = x_ref[b:b+SIDE, b:b+SIDE] - product(right[0], right[0], TN)
        left = []
        if put_inverse is not None:
            for j in range(k):
                piece = product(inv2, split(x_ref[a:b, j*SIDE:(j+1)*SIDE]), NN)
                put_inverse(k, j, piece)
                left.append(split(piece))
            put_inverse(k, k, inverse)
            left.append(inv2)
        for i in range(k+1, count):
            side = right[i-k-1]
            at = slice(i*SIDE, (i+1)*SIDE)
            for j in range(max(i, k+2), count):
                to = slice(j*SIDE, (j+1)*SIDE)
                x_ref[at, to] = x_ref[at, to] - product(side, right[j-k-1], TN)
            for j in range(len(left)):
                to = slice(j*SIDE, (j+1)*SIDE)
                change = product(side, left[j], TN)
                x_ref[at, to] = -change if j == k else x_ref[at, to] - change


def corners(n):
    count = n // SIDE
    return [(i, j) for i in range(count) for j in range(i, count)]


def block_slice(i):
    return slice(i * SIDE, (i + 1) * SIDE)


def leaf_kernel(
    gram_ref, transfer_ref, rounded_ref, packed_ref, high_ref, low_ref, moved_ref, x_ref, path_ref, carried_ref
):
    n = x_ref.shape[0]
    half = n // 2
    levels = transfer_ref.shape[0]
    x_ref[...] = gram_ref[...]
    order = corners(n)
    empty = jnp.zeros((SIDE, SIDE), bf16)
    for i, j in order:
        if i != j:
            rounded_ref[block_slice(j), block_slice(i)] = empty
            high_ref[block_slice(i), block_slice(j)] = empty
            low_ref[block_slice(i), block_slice(j)] = empty

    def put_triangle(i, j, value):
        value = value.astype(bf16)
        rounded_ref[block_slice(i), block_slice(j)] = value
        packed_ref[block_slice(order.index((i, j))), :] = value

    def put_inverse(i, j, value):
        high_ref[block_slice(i), block_slice(j)], low_ref[block_slice(i), block_slice(j)] = split(value)

    def beside(k, count):
        if k == 0:
            path = split(dot(transfer_ref[levels - 1], transfer_ref[levels - 2], TT))
            for level in reversed(range(levels - 2)):
                step = transfer_ref[level]
                path = split(dot(path[0], step, NT) + dot(path[1], step, NT))
            path_ref[0], path_ref[1] = path
        elif k == 1:
            carried_ref[0], carried_ref[1] = split(product((path_ref[0], path_ref[1]), split(gram_ref[...]), NN))
        elif k == 2:
            top, low = slice(0, half), slice(half, n)
            upper = product((path_ref[0, top], path_ref[1, top]), (carried_ref[0], carried_ref[1]), NT)
            lower = product((path_ref[0, low], path_ref[1, low]), (carried_ref[0, low], carried_ref[1, low]), NT)
            most = jnp.maximum(
                jnp.max(upper[:, :half], axis=(0, 1), keepdims=True), jnp.max(lower, axis=(0, 1), keepdims=True)
            )
            exponent = jnp.broadcast_to(jnp.ceil(jnp.log2(most)) - 13.0, (8, SIDE))
            shrink = jnp.exp2(-exponent)
            sub = lax.broadcasted_iota(jnp.int32, (8, SIDE), 0)
            lane = lax.broadcasted_iota(jnp.int32, (8, SIDE), 1)
            for number, (i, j) in enumerate(order):
                for p in range(SIDE // 8):
                    row = i * SIDE + 8 * p
                    if row < half:
                        piece = upper[row : row + 8, block_slice(j)]
                    else:
                        piece = lower[row - half : row - half + 8, j * SIDE - half : (j + 1) * SIDE - half]
                    piece = piece * shrink
                    if number == 0:
                        piece = jnp.where((sub == 7) & (lane == 0), exponent, piece)
                    moved_ref[p, 8 * number : 8 * number + 8, :] = piece

    factor(x_ref, put_triangle, put_inverse, beside)


def root_kernel(pieces_ref, high_ref, low_ref, basis_ref, root_ref, q_ref, x_ref):
    n = x_ref.shape[0]
    empty = jnp.zeros((SIDE, SIDE), bf16)
    for number, (i, j) in enumerate(corners(n)):
        for p in range(SIDE // 8):
            at = slice(i * SIDE + 8 * p, i * SIDE + 8 * p + 8)
            x_ref[at, block_slice(j)] = pieces_ref[p, 8 * number : 8 * number + 8, :]
        if i != j:
            root_ref[block_slice(j), block_slice(i)] = empty
    first = x_ref[:SIDE, :SIDE]
    sub = lax.broadcasted_iota(jnp.int32, first.shape, 0)
    lane = lax.broadcasted_iota(jnp.int32, first.shape, 1)
    x_ref[:SIDE, :SIDE] = jnp.where((lane == 0) & (sub > 0), first.T, first)

    def put_triangle(i, j, value):
        root_ref[block_slice(i), block_slice(j)] = value.astype(bf16)

    half = n // 2

    def beside(k, count):
        rows = basis_ref.shape[0] // count
        at = slice(k * rows, (k + 1) * rows)
        for to, inner in ((slice(0, half), half), (slice(half, n), n)):
            part = basis_ref[at, :inner]
            q_ref[at, to] = (dot(part, high_ref[to, :inner], NT) + dot(part, low_ref[to, :inner], NT)).astype(bf16)

    factor(x_ref, put_triangle, None, beside)


def gram_kernel(basis_hbm, gram_ref, basis_ref, sems):
    parts, rows = basis_ref.shape[0], basis_ref.shape[1]
    loads = [
        pltpu.make_async_copy(basis_hbm.at[pl.ds(c * rows, rows), :], basis_ref.at[c], sems.at[c]) for c in range(parts)
    ]
    for load in loads:
        load.start()
    half = gram_ref.shape[0] // 2
    for c in range(parts):
        loads[c].wait()
        basis = basis_ref[c]
        upper = dot(basis[:, :half], basis, TN)
        lower = dot(basis[:, half:], basis[:, half:], TN)
        if c > 0:
            upper = gram_ref[:half, :] + upper
            lower = gram_ref[half:, half:] + lower
        gram_ref[:half, :] = upper
        gram_ref[half:, half:] = lower
    gram_ref[half:, :half] = gram_ref[:half, half:].T


def left_kernel(rounded_ref, block_hbm, left_hbm, block_ref, left_ref, sems):
    slots, n = block_ref.shape[0], block_ref.shape[1]
    half = n // 2
    loads = [pltpu.make_async_copy(block_hbm.at[k], block_ref.at[k], sems.at[0, k]) for k in range(slots)]
    stores = [pltpu.make_async_copy(left_ref.at[k], left_hbm.at[k], sems.at[1, k]) for k in range(slots)]
    for load in loads:
        load.start()
    for k in range(slots):
        loads[k].wait()
        left_ref[k, :half, :] = dot(rounded_ref[:half, :], block_ref[k], NN).astype(bf16)
        left_ref[k, half:, :] = dot(rounded_ref[half:, half:], block_ref[k, half:, :], NN).astype(bf16)
        stores[k].start()
    for store in stores:
        store.wait()


def right_kernel(pick_ref, left_hbm, mine_hbm, other_hbm, out_hbm, left_ref, chosen_ref, out_ref, sems):
    slots, n = left_ref.shape[0], left_ref.shape[1]
    half = n // 2
    chips = mine_hbm.shape[0]
    here = lax.axis_index("col")
    for k in range(slots):
        pick = pick_ref[k]
        place = ((pick >> 1) - (here >> 1)) & (chips - 1)
        swapped = ((pick ^ here) & 1) != 0
        pltpu.make_async_copy(left_hbm.at[k], left_ref.at[k], sems.at[0, k]).start()

        @pl.when(swapped)
        def _():
            pltpu.make_async_copy(other_hbm.at[place], chosen_ref.at[k], sems.at[1, k]).start()

        @pl.when(jnp.logical_not(swapped))
        def _():
            pltpu.make_async_copy(mine_hbm.at[place], chosen_ref.at[k], sems.at[1, k]).start()

    order = corners(n)
    empty = jnp.zeros((SIDE, SIDE), bf16)
    stores = []
    for k in range(slots):
        pltpu.make_async_copy(left_hbm.at[k], left_ref.at[k], sems.at[0, k]).wait()
        pltpu.make_async_copy(mine_hbm.at[0], chosen_ref.at[k], sems.at[1, k]).wait()

        def row(i, start):
            blocks = [
                chosen_ref[k, block_slice(order.index((i, j))), :] if j >= i else empty
                for j in range(start, n // SIDE)
            ]
            return jnp.concatenate(blocks, axis=1)

        count = n // SIDE
        above = jnp.concatenate([row(i, 0) for i in range(count // 2)], axis=0)
        below = jnp.concatenate([row(i, count // 2) for i in range(count // 2, count)], axis=0)
        out_ref[k, :, :half] = dot(left_ref[k], above, NT).astype(bf16)
        out_ref[k, :, half:] = dot(left_ref[k, :, half:], below, NT).astype(bf16)
        stores.append(pltpu.make_async_copy(out_ref.at[k], out_hbm.at[k], sems.at[2, k]))
        stores[k].start()
    for store in stores:
        store.wait()


def shards(leaf_basis, transfers, couplings, partners):
    basis, steps, blocks, picks = leaf_basis[0, 0], transfers[0, 0], couplings[0, 0], partners[0, 0]
    leaf, rank = basis.shape
    levels = steps.shape[0]
    slots = blocks.shape[0]
    square = lambda dtype: jax.ShapeDtypeStruct((rank, rank), dtype)
    tall = len(corners(rank)) * SIDE
    work = pltpu.VMEM((rank, rank), f32)
    far = pl.BlockSpec(memory_space=pl.ANY)
    near = pl.BlockSpec(memory_space=pltpu.VMEM)
    group = 1 << levels
    share_shape = (SIDE // 8, tall * 8 // SIDE, SIDE)
    parts = 4
    gram = pl.pallas_call(
        gram_kernel,
        out_shape=square(f32),
        in_specs=[far],
        out_specs=near,
        scratch_shapes=[pltpu.VMEM((parts, leaf // parts, rank), bf16), pltpu.SemaphoreType.DMA((parts,))],
        name="gram",
    )(basis)
    pair = pltpu.VMEM((2, rank, rank), bf16)
    rounded, packed, high, low, moved = pl.pallas_call(
        leaf_kernel,
        out_shape=(
            square(bf16),
            jax.ShapeDtypeStruct((tall, SIDE), bf16),
            square(bf16),
            square(bf16),
            jax.ShapeDtypeStruct(share_shape, f32),
        ),
        scratch_shapes=[work, pair, pair],
        name="leaf",
    )(gram, steps)

    count = lax.axis_size("sub")
    groups = [list(range(low_end, low_end + group)) for low_end in range(0, count, group)]
    shares = lax.all_to_all(moved.astype(jnp.float16), "sub", 0, 0, axis_index_groups=groups)
    columns = lax.axis_size("col")
    mine = [packed]
    for shift in range(2, columns, 2):
        mine.append(lax.ppermute(packed, "col", [(i, (i - shift) % columns) for i in range(columns)]))
    exponents = shares[:, 7, 0].astype(f32)
    common = jnp.max(exponents) + 4.0
    share = jnp.sum(shares.astype(f32) * jnp.exp2(exponents - common)[:, None, None], axis=0).astype(jnp.float16)
    share, rounded = lax.optimization_barrier((share, rounded))
    top = lax.all_to_all(jnp.broadcast_to(share, shares.shape), "sub", 0, 0, axis_index_groups=groups)
    left = pl.pallas_call(
        left_kernel,
        out_shape=jax.ShapeDtypeStruct(blocks.shape, bf16),
        in_specs=[near, far],
        out_specs=far,
        scratch_shapes=[
            pltpu.VMEM(blocks.shape, bf16),
            pltpu.VMEM(blocks.shape, bf16),
            pltpu.SemaphoreType.DMA((2, slots)),
        ],
        name="left",
    )(rounded, blocks)
    mine, left = lax.optimization_barrier((tuple(mine), left))
    mine = jnp.stack(mine)
    other = lax.ppermute(mine, "col", [(i, i ^ 1) for i in range(columns)])
    top, mine, left = lax.optimization_barrier((top, mine, left))
    top = top.astype(f32) * jnp.exp2(common)
    root, q_leaf = pl.pallas_call(
        root_kernel,
        out_shape=(square(bf16), jax.ShapeDtypeStruct(basis.shape, bf16)),
        scratch_shapes=[work],
        name="root",
    )(top, high, low, basis)
    left, other, root, q_leaf = lax.optimization_barrier((left, other, root, q_leaf))
    coupled = pl.pallas_call(
        right_kernel,
        out_shape=jax.ShapeDtypeStruct(blocks.shape, bf16),
        in_specs=[pl.BlockSpec(memory_space=pltpu.SMEM), far, far, far],
        out_specs=far,
        scratch_shapes=[
            pltpu.VMEM(blocks.shape, bf16),
            pltpu.VMEM((slots, tall, SIDE), bf16),
            pltpu.VMEM(blocks.shape, bf16),
            pltpu.SemaphoreType.DMA((3, slots)),
        ],
        compiler_params=pltpu.CompilerParams(vmem_limit_bytes=24 << 20),
        name="right",
    )(picks, left, mine, other)
    return (q_leaf[None, None], root[None, None], coupled[None, None])


def solution(mesh):
    in_specs = (
        P("sub", "col", None, None),
        P("sub", "col", None, None, None),
        P("sub", "col", None, None, None),
        P("sub", "col", None),
    )
    out_specs = (
        P("sub", "col", None, None),
        P("sub", "col", None, None),
        P("sub", "col", None, None, None),
    )
    return jax.shard_map(shards, mesh=mesh, in_specs=in_specs, out_specs=out_specs, check_vma=False)
```

```python
import jax
import jax.numpy as jnp
from jax import lax
from jax.experimental import pallas as pl
from jax.experimental.pallas import tpu as pltpu
from jax.sharding import PartitionSpec as P


f32, bf16 = jnp.float32, jnp.bfloat16
NN = ((1,), (0,))
TN = ((0,), (0,))
NT = ((1,), (1,))
TT = ((0,), (1,))
SIDE = 128


def split(a):
    high = a.astype(bf16)
    return high, (a - high.astype(f32)).astype(bf16)


def dot(a, b, dims):
    return lax.dot_general(a, b, (dims, ((), ())), preferred_element_type=f32)


def product(a, b, dims):
    return dot(a[0], b[0], dims) + (dot(a[0], b[1], dims) + dot(a[1], b[0], dims))


def lane_of(rows, column):
    return jnp.take_along_axis(rows, jnp.full(rows.shape, column, jnp.int32), axis=1)


def invert_lower(block):
    n = block.shape[0]; parts = n // 8
    lane = lax.broadcasted_iota(jnp.int32, (8, n), 1)
    sub = lax.broadcasted_iota(jnp.int32, (8, n), 0)
    rows = [block[8*t:8*t+8, :] for t in range(parts)]
    result = []
    wide = lambda v: jnp.broadcast_to(v, (8, n))

    def pivots(t):
        here = (lane >= 8*t) & (lane < 8*t + 8)
        cols = [lane_of(rows[t], 8*t+k) for k in range(8)]
        work = jnp.where(here, (lane == sub + 8*t).astype(f32), rows[t])
        done = jnp.zeros((8, n), f32); scale = jnp.zeros((8, n), f32)
        for j in range(8):
            root = lax.rsqrt(wide(cols[j][j:j+1, :]))
            factor = jnp.where(sub == j, 0.0, cols[j]) * root
            for k in range(j+1, 8):
                cols[k] = cols[k] - factor * (wide(cols[k][j:j+1, :]) * root)
            pivot = wide(work[j:j+1, :]) * root
            done = jnp.where(sub == j, pivot, done)
            scale = jnp.where(sub == j, root * root, scale)
            work = work - factor * pivot
        result.append(jnp.where(lane < 8*t + 8, done, 0.0))
        rows[t] = work * scale
        return here, [wide(rows[t][k:k+1, :]) for k in range(8)]

    def apply(s, t, here, lines):
        terms = [lane_of(rows[s], 8*t+k) * lines[k] for k in range(8)]
        a = (terms[0] + terms[1]) + (terms[2] + terms[3])
        b = (terms[4] + terms[5]) + (terms[6] + terms[7])
        rows[s] = jnp.where(here, 0.0, rows[s]) - (a + b)

    for t in range(0, parts, 2):
        here, lines = pivots(t)
        apply(t+1, t, here, lines)
        more = t + 2 < parts
        if more: apply(t+2, t, here, lines)
        here, lines = pivots(t+1)
        if more:
            apply(t+2, t+1, here, lines)
            apply(t, t+1, here, lines)
        if t + 3 < parts:
            low, high = 8*t, 8*t+16
            solved = jnp.concatenate([rows[t], rows[t+1]], axis=0)
            rest = jnp.concatenate(rows[t+3:], axis=0)
            ln = lax.broadcasted_iota(jnp.int32, rest.shape, 1)
            change = product(split(rest[:, low:high]), split(solved), NN)
            rest = jnp.where((ln >= low) & (ln < high), 0.0, rest) - change
            for i in range(t+3, parts):
                rows[i] = rest[8*(i-t-3):8*(i-t-3)+8, :]
    return jnp.concatenate(result, axis=0)


def factor(x_ref, put_triangle, put_inverse, beside=None, first=0, last=None):
    n = x_ref.shape[0]; count = n // SIDE
    sub = lax.broadcasted_iota(jnp.int32, (SIDE, SIDE), 0)
    lane = lax.broadcasted_iota(jnp.int32, (SIDE, SIDE), 1)
    last = count if last is None else last
    diagonal = x_ref[first*SIDE:(first+1)*SIDE, first*SIDE:(first+1)*SIDE]
    for k in range(first, last):
        a, b = k*SIDE, (k+1)*SIDE
        if beside is not None:
            beside(k, count)
        inverse = invert_lower(diagonal)
        inv2 = split(inverse)
        put_triangle(k, k, jnp.where(lane >= sub, product(inv2, split(diagonal), NN), 0.0))
        right = []
        for j in range(k+1, count):
            piece = product(inv2, split(x_ref[a:b, j*SIDE:(j+1)*SIDE]), NN)
            put_triangle(k, j, piece)
            right.append(split(piece))
            if j == k+1:
                diagonal = x_ref[b:b+SIDE, b:b+SIDE] - product(right[0], right[0], TN)
                if j == last:
                    x_ref[b:b+SIDE, b:b+SIDE] = diagonal
        left = []
        if put_inverse is not None:
            for j in range(k):
                piece = product(inv2, split(x_ref[a:b, j*SIDE:(j+1)*SIDE]), NN)
                put_inverse(k, j, piece)
                left.append(split(piece))
            put_inverse(k, k, inverse)
            left.append(inv2)
        for i in range(k+1, count):
            side = right[i-k-1]
            at = slice(i*SIDE, (i+1)*SIDE)
            for j in range(max(i, k+2), count):
                to = slice(j*SIDE, (j+1)*SIDE)
                x_ref[at, to] = x_ref[at, to] - product(side, right[j-k-1], TN)
            for j in range(len(left)):
                to = slice(j*SIDE, (j+1)*SIDE)
                change = product(side, left[j], TN)
                x_ref[at, to] = -change if j == k else x_ref[at, to] - change


def corners(n):
    count = n // SIDE
    return [(i, j) for i in range(count) for j in range(i, count)]


def block_slice(i):
    return slice(i * SIDE, (i + 1) * SIDE)


def first_kernel(
    gram_ref, transfer_ref, rounded_ref, packed_ref, high_ref, low_ref, moved_ref, state_ref, x_ref, path_ref, carried_ref
):
    n = x_ref.shape[0]
    half = n // 2
    levels = transfer_ref.shape[0]
    x_ref[...] = gram_ref[...]
    order = corners(n)
    empty = jnp.zeros((SIDE, SIDE), bf16)
    rounded_ref[block_slice(1), block_slice(0)] = empty
    high_ref[block_slice(0), block_slice(1)] = empty
    low_ref[block_slice(0), block_slice(1)] = empty

    def put_triangle(i, j, value):
        value = value.astype(bf16)
        rounded_ref[block_slice(i), block_slice(j)] = value
        packed_ref[block_slice(order.index((i, j))), :] = value

    def put_inverse(i, j, value):
        high_ref[block_slice(i), block_slice(j)], low_ref[block_slice(i), block_slice(j)] = split(value)

    def beside(k, count):
        if k == 0:
            path = split(dot(transfer_ref[levels - 1], transfer_ref[levels - 2], TT))
            for level in reversed(range(levels - 2)):
                step = transfer_ref[level]
                path = split(dot(path[0], step, NT) + dot(path[1], step, NT))
            path_ref[0], path_ref[1] = path
            carried_ref[0], carried_ref[1] = split(product((path_ref[0], path_ref[1]), split(gram_ref[...]), NN))
        elif k == 1:
            top, low = slice(0, half), slice(half, n)
            upper = product((path_ref[0, top], path_ref[1, top]), (carried_ref[0], carried_ref[1]), NT)
            lower = product((path_ref[0, low], path_ref[1, low]), (carried_ref[0, low], carried_ref[1, low]), NT)
            most = jnp.maximum(
                jnp.max(upper[:, :half], axis=(0, 1), keepdims=True), jnp.max(lower, axis=(0, 1), keepdims=True)
            )
            exponent = jnp.broadcast_to(jnp.ceil(jnp.log2(most)) - 13.0, (8, SIDE))
            shrink = jnp.exp2(-exponent)
            sub = lax.broadcasted_iota(jnp.int32, (8, SIDE), 0)
            lane = lax.broadcasted_iota(jnp.int32, (8, SIDE), 1)
            for number, (i, j) in enumerate(order):
                for p in range(SIDE // 8):
                    row = i * SIDE + 8 * p
                    if row < half:
                        piece = upper[row : row + 8, block_slice(j)]
                    else:
                        piece = lower[row - half : row - half + 8, j * SIDE - half : (j + 1) * SIDE - half]
                    piece = piece * shrink
                    if number == 0:
                        piece = jnp.where((sub == 7) & (lane == 0), exponent, piece)
                    moved_ref[p, 8 * number : 8 * number + 8, :] = piece

    factor(x_ref, put_triangle, put_inverse, beside, last=n // SIDE // 2)
    state_ref[...] = x_ref[half:, :]


def second_kernel(state_ref, started_ref, rounded_ref, packed_ref, high_ref, low_ref, x_ref):
    n = x_ref.shape[0]
    half = n // 2
    middle = half // SIDE
    order = corners(n)
    x_ref[half:, :] = state_ref[...]
    packed_ref[: started_ref.shape[0], :] = started_ref[...]
    empty = jnp.zeros((SIDE, SIDE), bf16)
    rounded_ref[block_slice(1), block_slice(0)] = empty
    high_ref[block_slice(0), block_slice(middle + 1)] = empty
    low_ref[block_slice(0), block_slice(middle + 1)] = empty

    def put_triangle(i, j, value):
        value = value.astype(bf16)
        rounded_ref[block_slice(i - middle), block_slice(j - middle)] = value
        packed_ref[block_slice(order.index((i, j))), :] = value

    def put_inverse(i, j, value):
        at = block_slice(i - middle), block_slice(j)
        high_ref[at], low_ref[at] = split(value)

    factor(x_ref, put_triangle, put_inverse, first=middle)


def root_kernel(pieces_ref, high_ref, low_ref, next_high_ref, next_low_ref, basis_ref, root_ref, q_ref, x_ref):
    n = x_ref.shape[0]
    empty = jnp.zeros((SIDE, SIDE), bf16)
    for number, (i, j) in enumerate(corners(n)):
        for p in range(SIDE // 8):
            at = slice(i * SIDE + 8 * p, i * SIDE + 8 * p + 8)
            x_ref[at, block_slice(j)] = pieces_ref[p, 8 * number : 8 * number + 8, :]
        if i != j:
            root_ref[block_slice(j), block_slice(i)] = empty
    first = x_ref[:SIDE, :SIDE]
    sub = lax.broadcasted_iota(jnp.int32, first.shape, 0)
    lane = lax.broadcasted_iota(jnp.int32, first.shape, 1)
    x_ref[:SIDE, :SIDE] = jnp.where((lane == 0) & (sub > 0), first.T, first)

    def put_triangle(i, j, value):
        root_ref[block_slice(i), block_slice(j)] = value.astype(bf16)

    half = n // 2

    def beside(k, count):
        rows = basis_ref.shape[0] // count
        at = slice(k * rows, (k + 1) * rows)
        part = basis_ref[at, :half]
        q_ref[at, :half] = (dot(part, high_ref[...], NT) + dot(part, low_ref[...], NT)).astype(bf16)
        part = basis_ref[at, :]
        q_ref[at, half:] = (dot(part, next_high_ref[...], NT) + dot(part, next_low_ref[...], NT)).astype(bf16)

    factor(x_ref, put_triangle, None, beside)


def gram_kernel(basis_hbm, gram_ref, basis_ref, sems):
    parts, rows = basis_ref.shape[0], basis_ref.shape[1]
    loads = [
        pltpu.make_async_copy(basis_hbm.at[pl.ds(c * rows, rows), :], basis_ref.at[c], sems.at[c]) for c in range(parts)
    ]
    for load in loads:
        load.start()
    half = gram_ref.shape[0] // 2
    for c in range(parts):
        loads[c].wait()
        basis = basis_ref[c]
        upper = dot(basis[:, :half], basis, TN)
        lower = dot(basis[:, half:], basis[:, half:], TN)
        if c > 0:
            upper = gram_ref[:half, :] + upper
            lower = gram_ref[half:, half:] + lower
        gram_ref[:half, :] = upper
        gram_ref[half:, half:] = lower
    gram_ref[half:, :half] = gram_ref[:half, half:].T


def left_kernel(rounded_ref, next_ref, block_hbm, left_hbm, block_ref, left_ref, sems):
    slots, n = block_ref.shape[0], block_ref.shape[1]
    half = n // 2
    loads = [pltpu.make_async_copy(block_hbm.at[k], block_ref.at[k], sems.at[0, k]) for k in range(slots)]
    stores = [pltpu.make_async_copy(left_ref.at[k], left_hbm.at[k], sems.at[1, k]) for k in range(slots)]
    for load in loads:
        load.start()
    for k in range(slots):
        loads[k].wait()
        left_ref[k, :half, :] = dot(rounded_ref[...], block_ref[k], NN).astype(bf16)
        left_ref[k, half:, :] = dot(next_ref[...], block_ref[k, half:, :], NN).astype(bf16)
        stores[k].start()
    for store in stores:
        store.wait()


def right_kernel(pick_ref, left_hbm, mine_hbm, other_hbm, out_hbm, left_ref, chosen_ref, out_ref, sems):
    slots, n = left_ref.shape[0], left_ref.shape[1]
    half = n // 2
    chips = mine_hbm.shape[0]
    here = lax.axis_index("col")
    for k in range(slots):
        pick = pick_ref[k]
        place = ((pick >> 1) - (here >> 1)) & (chips - 1)
        swapped = ((pick ^ here) & 1) != 0
        pltpu.make_async_copy(left_hbm.at[k], left_ref.at[k], sems.at[0, k]).start()

        @pl.when(swapped)
        def _():
            pltpu.make_async_copy(other_hbm.at[place], chosen_ref.at[k], sems.at[1, k]).start()

        @pl.when(jnp.logical_not(swapped))
        def _():
            pltpu.make_async_copy(mine_hbm.at[place], chosen_ref.at[k], sems.at[1, k]).start()

    order = corners(n)
    empty = jnp.zeros((SIDE, SIDE), bf16)
    stores = []
    for k in range(slots):
        pltpu.make_async_copy(left_hbm.at[k], left_ref.at[k], sems.at[0, k]).wait()
        pltpu.make_async_copy(mine_hbm.at[0], chosen_ref.at[k], sems.at[1, k]).wait()

        def row(i, start):
            blocks = [
                chosen_ref[k, block_slice(order.index((i, j))), :] if j >= i else empty
                for j in range(start, n // SIDE)
            ]
            return jnp.concatenate(blocks, axis=1)

        count = n // SIDE
        above = jnp.concatenate([row(i, 0) for i in range(count // 2)], axis=0)
        below = jnp.concatenate([row(i, count // 2) for i in range(count // 2, count)], axis=0)
        out_ref[k, :, :half] = dot(left_ref[k], above, NT).astype(bf16)
        out_ref[k, :, half:] = dot(left_ref[k, :, half:], below, NT).astype(bf16)
        stores.append(pltpu.make_async_copy(out_ref.at[k], out_hbm.at[k], sems.at[2, k]))
        stores[k].start()
    for store in stores:
        store.wait()


def shards(leaf_basis, transfers, couplings, partners):
    basis, steps, blocks, picks = leaf_basis[0, 0], transfers[0, 0], couplings[0, 0], partners[0, 0]
    leaf, rank = basis.shape
    levels = steps.shape[0]
    slots = blocks.shape[0]
    square = lambda dtype: jax.ShapeDtypeStruct((rank, rank), dtype)
    tall = len(corners(rank)) * SIDE
    work = pltpu.VMEM((rank, rank), f32)
    far = pl.BlockSpec(memory_space=pl.ANY)
    near = pl.BlockSpec(memory_space=pltpu.VMEM)
    group = 1 << levels
    share_shape = (SIDE // 8, tall * 8 // SIDE, SIDE)
    parts = 4
    gram = pl.pallas_call(
        gram_kernel,
        out_shape=square(f32),
        in_specs=[far],
        out_specs=near,
        scratch_shapes=[pltpu.VMEM((parts, leaf // parts, rank), bf16), pltpu.SemaphoreType.DMA((parts,))],
        name="gram",
    )(basis)
    pair = pltpu.VMEM((2, rank, rank), bf16)
    half = rank // 2
    grid = lambda rows, columns, dtype: jax.ShapeDtypeStruct((rows, columns), dtype)
    rounded, packed, high, low, moved, state = pl.pallas_call(
        first_kernel,
        out_shape=(
            grid(half, rank, bf16),
            grid(sum(i * SIDE < half for i, _ in corners(rank)) * SIDE, SIDE, bf16),
            grid(half, half, bf16),
            grid(half, half, bf16),
            jax.ShapeDtypeStruct(share_shape, f32),
            grid(half, rank, f32),
        ),
        scratch_shapes=[work, pair, pair],
        name="first",
    )(gram, steps)

    count = lax.axis_size("sub")
    groups = [list(range(low_end, low_end + group)) for low_end in range(0, count, group)]
    shares = lax.all_to_all(moved.astype(jnp.float16), "sub", 0, 0, axis_index_groups=groups)
    next_rounded, packed, next_high, next_low = pl.pallas_call(
        second_kernel,
        out_shape=(grid(half, half, bf16), grid(tall, SIDE, bf16), grid(half, rank, bf16), grid(half, rank, bf16)),
        scratch_shapes=[work],
        name="second",
    )(state, packed)
    shares, packed, next_rounded, next_high, next_low = lax.optimization_barrier(
        (shares, packed, next_rounded, next_high, next_low)
    )
    columns = lax.axis_size("col")
    mine = [packed]
    for shift in range(2, columns, 2):
        mine.append(lax.ppermute(packed, "col", [(i, (i - shift) % columns) for i in range(columns)]))
    exponents = shares[:, 7, 0].astype(f32)
    common = jnp.max(exponents) + 4.0
    share = jnp.sum(shares.astype(f32) * jnp.exp2(exponents - common)[:, None, None], axis=0).astype(jnp.float16)
    share, rounded = lax.optimization_barrier((share, rounded))
    top = lax.all_to_all(jnp.broadcast_to(share, shares.shape), "sub", 0, 0, axis_index_groups=groups)
    left = pl.pallas_call(
        left_kernel,
        out_shape=jax.ShapeDtypeStruct(blocks.shape, bf16),
        in_specs=[near, near, far],
        out_specs=far,
        scratch_shapes=[
            pltpu.VMEM(blocks.shape, bf16),
            pltpu.VMEM(blocks.shape, bf16),
            pltpu.SemaphoreType.DMA((2, slots)),
        ],
        name="left",
    )(rounded, next_rounded, blocks)
    mine, left = lax.optimization_barrier((tuple(mine), left))
    mine = jnp.stack(mine)
    other = lax.ppermute(mine, "col", [(i, i ^ 1) for i in range(columns)])
    top, mine, left = lax.optimization_barrier((top, mine, left))
    top = top.astype(f32) * jnp.exp2(common)
    root, q_leaf = pl.pallas_call(
        root_kernel,
        out_shape=(square(bf16), jax.ShapeDtypeStruct(basis.shape, bf16)),
        scratch_shapes=[work],
        name="root",
    )(top, high, low, next_high, next_low, basis)
    left, other, root, q_leaf = lax.optimization_barrier((left, other, root, q_leaf))
    coupled = pl.pallas_call(
        right_kernel,
        out_shape=jax.ShapeDtypeStruct(blocks.shape, bf16),
        in_specs=[pl.BlockSpec(memory_space=pltpu.SMEM), far, far, far],
        out_specs=far,
        scratch_shapes=[
            pltpu.VMEM(blocks.shape, bf16),
            pltpu.VMEM((slots, tall, SIDE), bf16),
            pltpu.VMEM(blocks.shape, bf16),
            pltpu.SemaphoreType.DMA((3, slots)),
        ],
        compiler_params=pltpu.CompilerParams(vmem_limit_bytes=24 << 20),
        name="right",
    )(picks, left, mine, other)
    return (q_leaf[None, None], root[None, None], coupled[None, None])


def solution(mesh):
    in_specs = (
        P("sub", "col", None, None),
        P("sub", "col", None, None, None),
        P("sub", "col", None, None, None),
        P("sub", "col", None),
    )
    out_specs = (
        P("sub", "col", None, None),
        P("sub", "col", None, None),
        P("sub", "col", None, None, None),
    )
    return jax.shard_map(shards, mesh=mesh, in_specs=in_specs, out_specs=out_specs, check_vma=False)
```
